32 devices in a mesh: row: 16 (over z, y, x), col: 2 (over core).
Axes of the slice: x: 2, y: 2, z: 4, core: 2. Of those that a mesh axis runs over, the one named last changes fastest.
Arguments:
- panel_u: bfloat16 [16, 2560, 128], P('row'), may hold values from -0.125 to 0.125
- panel_v: bfloat16 [16, 2560, 128], P('row', 'col'), may hold values from -0.25 to 0.25
- linv: bfloat16 [2560, 2560], P('row', 'col')
- trail_u: bfloat16 [16, 4, 2560, 128], P('row', 'col'), may hold values from -0.125 to 0.125
- trail_v: bfloat16 [16, 4, 2560, 128], P('row', 'col'), may hold values from -0.125 to 0.125
- rank_map: int32 [16, 16], replicated, may hold values from 32 to 128, as said below
- tile_of_slot: int32 [16], replicated, may hold values from 0 to 15, each once
- band_cols: int32 [4], P('col'), may hold values from 0 to 15, as said below
Outputs:
- gram_left: float32 [16, 4, 256, 256], P('row', 'col')
- gram_right: float32 [16, 4, 256, 256], P('row', 'col')
The draws below stay inside these ranges and needn't reach their ends.
Inputs may be any that keep to these rules, and one draw needn't show every extreme that they name: rank_map[i, j] for j != i is the rank of trailing tile (i, j), including band tiles with j > i, whose core is zero; rank_map[i, i] is the rank of panel tile i; some panel tile has rank 128. `tile_of_slot`: a permutation. `band_cols`: distinct values.
All inputs are finite; a program needn't handle non-finite values.
Results may differ from the reference program's by a relative error of at most 0.0049.
Values may be sent and summed in bfloat16 or wider, within the bound.
No kernel may reach another device: no remote copies, remote signals or barrier semaphores. Data moves between devices by JAX's collectives and lax.ppermute only.
A program may use at most 64 MiB of HBM per device.

```python
import math
import jax
import jax.numpy as jnp
from jax import lax

B = 2560
R = 128
NT = 16
NC = 4


def draw_linv(key, part):
    diag_key, off_key = jax.random.split(jax.random.fold_in(key, 11))
    row_ids = jnp.arange(B)[:, None]
    col_ids = jnp.arange(B)[None, :]
    diagonal = jax.random.uniform(diag_key, (B, B), jnp.float32, 0.5, 1.5)
    spread = jax.random.normal(off_key, (B, B), jnp.float32)
    lower = jnp.where(row_ids > col_ids, spread * (1.0 / math.sqrt(B)), 0.0)
    return jnp.where(row_ids == col_ids, diagonal, lower).astype(jnp.bfloat16)


def draw_rank_map(key, part):
    value_key, spot_key = jax.random.split(jax.random.fold_in(key, 23))
    ranks = jax.random.randint(value_key, (NT, NT), R // 4, R + 1)
    spot = jax.random.randint(spot_key, (), 0, NT)
    tile_ids = jnp.arange(NT)
    on_spot = (tile_ids[:, None] == spot) & (tile_ids[None, :] == spot)
    return jnp.where(on_spot, R, ranks).astype(jnp.int32)


def draw_band_cols(key, part):
    order = jax.random.permutation(jax.random.fold_in(key, 37), NT)
    return order[:NC].astype(jnp.int32)


def levels(stream_key, dims, cuts, least, high):
    factor_of, own = 1.0, jax.random.fold_in(stream_key, 6)
    for axis_at, shards_of in cuts:
        steps = jnp.exp(jax.random.uniform(jax.random.fold_in(own, axis_at), (shards_of,), jnp.float32, least / len(cuts), high / len(cuts)))
        factor_of = factor_of * jnp.repeat(steps, dims[axis_at] // shards_of).reshape([-1 if axis == axis_at else 1 for axis in range(len(dims))])
    return factor_of


def noise(key, shape, scale, most, cuts=(), kind=jnp.bfloat16):
    values = jax.random.normal(key, shape, jnp.float32) * scale
    if len(cuts) > 0:
        values = levels(key, shape, cuts, -0.22, 0.18) * values
    return jnp.clip(values, min=-most, max=most).astype(kind)


def setup_inputs(seed: int = 0) -> dict:
    streams_of = jax.random.split(jax.random.key(seed), 9)
    return {
        "panel_u": noise(streams_of[0], (NT, B, R), B ** -0.5, 0.125, ((0, 16),)),
        "panel_v": noise(streams_of[1], (NT, B, R), ((B * R) ** 0.5) ** -0.5, 0.25, ((0, 16), (1, 2))),
        "linv": draw_linv(jax.random.fold_in(streams_of[8], 71), 0),
        "trail_u": noise(streams_of[3], (NT, NC, B, R), B ** -0.5, 0.125, ((0, 16), (1, 2))),
        "trail_v": noise(streams_of[4], (NT, NC, B, R), B ** -0.5, 0.125, ((0, 16), (1, 2))),
        "rank_map": draw_rank_map(jax.random.fold_in(streams_of[8], 71), 0),
        "tile_of_slot": jax.random.permutation(streams_of[6], NT).astype(jnp.int32),
        "band_cols": draw_band_cols(jax.random.fold_in(streams_of[8], 71), 0),
    }


def reference(panel_u, panel_v, linv, trail_u, trail_v, rank_map, tile_of_slot, band_cols):
    columns = jnp.arange(R, dtype=jnp.int32)
    slot_ids = jnp.arange(NT, dtype=jnp.int32)
    diag_rank = jnp.sum(jnp.where(slot_ids[:, None] == slot_ids[None, :], rank_map, 0), axis=1)
    slot_rank = jnp.sum(jnp.where(tile_of_slot[:, None] == slot_ids[None, :], diag_rank[None, :], 0), axis=1)
    kept_cols = columns[None, None, :] < slot_rank[:, None, None]
    masked_u = jnp.where(kept_cols, panel_u, jnp.zeros_like(panel_u))
    masked_v = jnp.where(kept_cols, panel_v, jnp.zeros_like(panel_v))

    def solve_factor(factor):
        return jnp.dot(linv, factor, preferred_element_type=jnp.float32).astype(jnp.bfloat16)

    solved = lax.map(solve_factor, masked_v)
    slot_of_tile = jnp.sum(jnp.where(tile_of_slot[None, :] == slot_ids[:, None], slot_ids[None, :], 0), axis=1)

    def one_tile(tile_pair):
        slot_now = tile_pair[0]
        band_now = tile_pair[1]
        own_tile = tile_of_slot[slot_now]
        band_tile = band_cols[band_now]
        source = slot_of_tile[band_tile]
        core_mat = jnp.dot(solved[slot_now].T, solved[source], preferred_element_type=jnp.float32)
        core_mat = jnp.where(band_tile < own_tile, core_mat, jnp.zeros_like(core_mat)).astype(jnp.bfloat16)
        update = jnp.dot(masked_u[source], core_mat.T, preferred_element_type=jnp.float32).astype(jnp.bfloat16)
        trail_keep = columns[None, :] < rank_map[own_tile, band_tile]
        kept_u = jnp.where(trail_keep, trail_u[slot_now, band_now], jnp.zeros_like(update))
        kept_v = jnp.where(trail_keep, trail_v[slot_now, band_now], jnp.zeros_like(update))
        left_stack = jnp.concatenate([kept_u, masked_u[slot_now]], axis=1)
        right_stack = jnp.concatenate([kept_v, -update], axis=1)
        left_gram = jnp.dot(left_stack.T, left_stack, preferred_element_type=jnp.float32)
        right_gram = jnp.dot(right_stack.T, right_stack, preferred_element_type=jnp.float32)
        return left_gram, right_gram

    slot_grid = jnp.repeat(slot_ids, NC)
    band_grid = jnp.tile(jnp.arange(NC, dtype=jnp.int32), NT)
    tile_pairs = jnp.stack([slot_grid, band_grid], axis=1).astype(jnp.int32)
    left_grams, right_grams = lax.map(one_tile, tile_pairs)
    return left_grams.reshape(NT, NC, 2 * R, 2 * R), right_grams.reshape(NT, NC, 2 * R, 2 * R)
```

```python
import functools

import jax
import jax.numpy as jnp
from jax import lax
from jax.experimental import pallas as pl
from jax.experimental.pallas import tpu as pltpu
from jax.sharding import PartitionSpec as P


VMEM = pl.BlockSpec(memory_space=pltpu.VMEM)
SMEM = pl.BlockSpec(memory_space=pltpu.SMEM)


def cross_rows(first, second):
    return lax.dot_general(
        first, second, (((0,), (0,)), ((), ())), preferred_element_type=jnp.float32
    )


def slot_of(tiles_ref, tile):
    slot = jnp.int32(0)
    for s in range(tiles_ref.shape[0]):
        slot = jnp.where(tiles_ref[s] == tile, jnp.int32(s), slot)
    return slot


def keep_mask(width, first_rank, second_rank):
    rows = lax.broadcasted_iota(jnp.int32, (2 * width, 2 * width), 0)
    cols = lax.broadcasted_iota(jnp.int32, (2 * width, 2 * width), 1)

    def kept(ids):
        return ids < jnp.where(ids < width, first_rank, second_rank + width)

    return kept(rows) & kept(cols)


def solve_kernel(ids_ref, *refs, inner, cols):
    outer = len(refs) - cols - inner
    l_refs, v_refs, out_refs = refs[:inner], refs[inner : len(refs) - cols], refs[-cols:]
    per_col = inner // cols
    low, core = ids_ref[1], ids_ref[2]
    factors = jnp.concatenate([ref[...] for ref in v_refs], axis=1)
    rows = l_refs[0].shape[0]
    for k in range(inner):
        value = jnp.dot(l_refs[k][...], factors, preferred_element_type=jnp.float32)
        block = low ^ k
        owner = (block // per_col) ^ core
        at = pl.multiple_of((block % per_col) * rows, 8)
        for j in range(cols):

            @pl.when(owner == j)
            def _():
                out_refs[j][pl.ds(at, rows), :] = value


def core_kernel(ids_ref, tiles_ref, *refs, inner, cols, width):
    bands_refs, s_refs, out_refs = refs[:cols], refs[cols : cols + inner], refs[cols + inner : -1]
    picked = refs[-1]
    high, low = ids_ref[0], ids_ref[1]
    per_col = bands_refs[0].shape[0]
    for j in range(cols):
        for b in range(per_col):
            source = slot_of(tiles_ref, bands_refs[j][b])
            block = low ^ (source % inner)
            at = pl.multiple_of((high ^ (source // inner)) * width, width)
            place = (j * per_col + b) * width
            for k in range(inner):

                @pl.when(block == k)
                def _():
                    picked[:, place : place + width] = s_refs[k][:, pl.ds(at, width)]

    own = s_refs[0][...]
    for j in range(cols):
        out_refs[j][...] = cross_rows(
            own, picked[:, j * per_col * width : (j + 1) * per_col * width]
        )


def left_kernel(ids_ref, tiles_ref, ranks_ref, bands_ref, trail_ref, panel_ref, out_ref, *, width):
    own_tile = tiles_ref[ids_ref[3]]
    own_rank = ranks_ref[own_tile, own_tile]
    for b in range(bands_ref.shape[0]):
        stack = jnp.concatenate([trail_ref[0, b], panel_ref[0]], axis=1)
        mask = keep_mask(width, ranks_ref[own_tile, bands_ref[b]], own_rank)
        out_ref[0, b] = jnp.where(mask, cross_rows(stack, stack), 0.0)


def pick_kernel(ids_ref, tiles_ref, bands_ref, *refs, inner, outer):
    t_refs, out_refs = refs[:inner], refs[inner:]
    high, low = ids_ref[0], ids_ref[1]
    for b in range(bands_ref.shape[0]):
        block = low ^ (slot_of(tiles_ref, bands_ref[b]) % inner)
        for k in range(inner):

            @pl.when(block == k)
            def _():
                for m in range(outer):
                    out_refs[m][b] = t_refs[k][high ^ m]


def merge_kernel(ids_ref, tiles_ref, bands_ref, *refs, inner, outer):
    r_refs, out_ref = refs[:outer], refs[outer]
    high = ids_ref[0]
    for b in range(bands_ref.shape[0]):
        block = high ^ (slot_of(tiles_ref, bands_ref[b]) // inner)
        for m in range(outer):

            @pl.when(block == m)
            def _():
                out_ref[b] = r_refs[m][b]


def right_kernel(ids_ref, tiles_ref, ranks_ref, bands_ref, *refs, inner, outer, width):
    part_refs = refs[:outer]
    q_refs = refs[outer : outer + inner]
    trail_ref, out_ref, stack = refs[outer + inner :]
    high, low = ids_ref[0], ids_ref[1]
    own_tile = tiles_ref[ids_ref[3]]
    own_rank = ranks_ref[own_tile, own_tile]
    sub = q_refs[0].shape[2]
    rows = lax.broadcasted_iota(jnp.int32, (width, width), 0)
    cols = lax.broadcasted_iota(jnp.int32, (width, width), 1)
    for b in range(bands_ref.shape[0]):
        band_tile = bands_ref[b]
        lanes = slice(b * width, (b + 1) * width)
        total = part_refs[0][:, lanes]
        for m in range(1, outer):
            total = total + part_refs[m][:, lanes]
        live = (rows < own_rank) & (cols < ranks_ref[band_tile, band_tile])
        live = live & (band_tile < own_tile)
        core_mat = jnp.where(live, total, 0.0).astype(jnp.bfloat16)
        for p in range(inner * outer):
            stack[p, :, :width] = trail_ref[0, b, p]
        for k in range(inner):
            for m in range(outer):
                update = lax.dot_general(
                    q_refs[k][m, b],
                    core_mat,
                    (((1,), (1,)), ((), ())),
                    preferred_element_type=jnp.float32,
                )
                stack[(low ^ k) * outer + (high ^ m), :, width:] = -update.astype(jnp.bfloat16)
        if sub % 16 == 0:
            flat = stack[...].reshape(inner * outer * sub, 2 * width)
            gram = cross_rows(flat, flat)
        else:
            gram = jnp.zeros((2 * width, 2 * width), jnp.float32)
            for p in range(inner * outer):
                gram = gram + cross_rows(stack[p], stack[p])
        mask = keep_mask(width, ranks_ref[own_tile, band_tile], width)
        out_ref[0, b] = jnp.where(mask, gram, 0.0)


def shards(panel_u, panel_v, linv, trail_u, trail_v, rank_map, tile_of_slot, band_cols, *, rows, cols):
    inner = 1
    while inner * inner < rows:
        inner *= 2
    outer = rows // inner
    points, width = panel_u.shape[1], panel_u.shape[2]
    per_col = band_cols.shape[0]
    quarter = points // inner
    sub = quarter // outer
    f32, bf16 = jnp.float32, jnp.bfloat16
    row = lax.axis_index("row").astype(jnp.int32)
    core = lax.axis_index("col").astype(jnp.int32)
    high, low = row // inner, row % inner
    ids = jnp.stack([high, low, core, row])

    def low_swap(x, k):
        return lax.ppermute(x, "row", [(r, r ^ k) for r in range(rows)]) if k else x

    def high_swap(x, m):
        return lax.ppermute(x, "row", [(r, r ^ (m * inner)) for r in range(rows)]) if m else x

    def core_swap(x, j):
        return lax.ppermute(x, "col", [(c, c ^ j) for c in range(cols)]) if j else x

    def shape(dims, kind):
        return jax.ShapeDtypeStruct(dims, kind)

    l_blocks = [low_swap(linv, k) for k in range(inner)]
    v_blocks = [high_swap(panel_v[0], m) for m in range(outer)]
    bands = [core_swap(band_cols, j) for j in range(cols)]

    gram_left = pl.pallas_call(
        functools.partial(left_kernel, width=width),
        out_shape=shape((1, per_col, 2 * width, 2 * width), f32),
        in_specs=[SMEM] * 4 + [VMEM] * 2,
        out_specs=VMEM,
        name="gram_left",
    )(ids, tile_of_slot, rank_map, band_cols, trail_u, panel_u)

    pieces = panel_u[0].reshape(inner, outer, sub, width)
    t_blocks = [
        low_swap(lax.dynamic_index_in_dim(pieces, low ^ k, 0, keepdims=False), k)
        for k in range(inner)
    ]
    sends = pl.pallas_call(
        functools.partial(pick_kernel, inner=inner, outer=outer),
        out_shape=[shape((per_col, sub, width), bf16)] * outer,
        in_specs=[SMEM] * 3 + [VMEM] * inner,
        out_specs=[VMEM] * outer,
        name="pick",
    )(ids, tile_of_slot, band_cols, *t_blocks)
    got = [high_swap(sends[m], m) for m in range(outer)]
    piece = pl.pallas_call(
        functools.partial(merge_kernel, inner=inner, outer=outer),
        out_shape=shape((per_col, sub, width), bf16),
        in_specs=[SMEM] * 3 + [VMEM] * outer,
        out_specs=VMEM,
        name="merge",
    )(ids, tile_of_slot, band_cols, *got)
    bases = jnp.stack([high_swap(piece, m) for m in range(outer)])
    base_blocks = [low_swap(bases, k) for k in range(inner)]

    block_rows = linv.shape[0]
    kept_rows = inner // cols * block_rows
    parts = pl.pallas_call(
        functools.partial(solve_kernel, inner=inner, cols=cols),
        out_shape=[shape((kept_rows, outer * width), f32)] * cols,
        in_specs=[SMEM] + [VMEM] * (inner + outer),
        out_specs=[VMEM] * cols,
        name="solve",
    )(ids, *l_blocks, *v_blocks)
    solved = parts[0]
    for j in range(1, cols):
        solved = solved + core_swap(parts[j], j)
    solved = solved.astype(bf16)
    s_blocks = [low_swap(solved, k) for k in range(inner)]
    cores = pl.pallas_call(
        functools.partial(core_kernel, inner=inner, cols=cols, width=width),
        out_shape=[shape((outer * width, per_col * width), f32)] * cols,
        in_specs=[SMEM] * (2 + cols) + [VMEM] * inner,
        out_specs=[VMEM] * cols,
        scratch_shapes=[pltpu.VMEM((kept_rows, cols * per_col * width), bf16)],
        name="core",
    )(ids, tile_of_slot, *bands, *s_blocks)
    core_sum = cores[0]
    for j in range(1, cols):
        core_sum = core_sum + core_swap(cores[j], j)
    core_parts = [high_swap(core_sum[m * width : (m + 1) * width], m) for m in range(outer)]

    gram_right = pl.pallas_call(
        functools.partial(right_kernel, inner=inner, outer=outer, width=width),
        out_shape=shape((1, per_col, 2 * width, 2 * width), f32),
        in_specs=[SMEM] * 4 + [VMEM] * (outer + inner + 1),
        out_specs=VMEM,
        scratch_shapes=[pltpu.VMEM((inner * outer, sub, 2 * width), bf16)],
        name="gram_right",
    )(
        ids,
        tile_of_slot,
        rank_map,
        band_cols,
        *core_parts,
        *base_blocks,
        trail_v.reshape(1, per_col, inner * outer, sub, width),
    )
    return gram_left, gram_right


def solution(mesh):
    return jax.shard_map(
        functools.partial(shards, rows=mesh.shape["row"], cols=mesh.shape["col"]),
        mesh=mesh,
        in_specs=(
            P("row", None, None),
            P("row", "col", None),
            P("row", "col"),
            P("row", "col", None, None),
            P("row", "col", None, None),
            P(),
            P(),
            P("col"),
        ),
        out_specs=(P("row", "col", None, None), P("row", "col", None, None)),
        check_vma=False,
    )
```

```python
import functools

import jax
import jax.numpy as jnp
from jax import lax
from jax.experimental import pallas as pl
from jax.experimental.pallas import tpu as pltpu
from jax.sharding import PartitionSpec as P


SCRATCH_BYTES = 16 * 1024 * 1024

VMEM = pl.BlockSpec(memory_space=pltpu.VMEM)
SMEM = pl.BlockSpec(memory_space=pltpu.SMEM)


def cross_rows(first, second):
    return lax.dot_general(
        first, second, (((0,), (0,)), ((), ())), preferred_element_type=jnp.float32
    )


def slot_of(tiles_ref, tile):
    slot = jnp.int32(0)
    for s in range(tiles_ref.shape[0]):
        slot = jnp.where(tiles_ref[s] == tile, jnp.int32(s), slot)
    return slot


def keep_mask(width, first_rank, second_rank):
    rows = lax.broadcasted_iota(jnp.int32, (2 * width, 2 * width), 0)
    cols = lax.broadcasted_iota(jnp.int32, (2 * width, 2 * width), 1)

    def kept(ids):
        return ids < jnp.where(ids < width, first_rank, second_rank + width)

    return kept(rows) & kept(cols)


def solve_kernel(ids_ref, *refs, pieces, cols):
    inner = len(pieces)
    count = sum(pieces)
    l_refs, v_refs, out_refs = refs[:count], refs[count : len(refs) - cols], refs[-cols:]
    per_col = inner // cols
    low, core = ids_ref[1], ids_ref[2]
    factors = jnp.concatenate([ref[...] for ref in v_refs], axis=1)
    rows = l_refs[0].shape[0]
    if rows % 16 == 0:
        lines = jnp.concatenate([ref[...] for ref in l_refs], axis=0)
        value = jnp.dot(lines, factors, preferred_element_type=jnp.float32)
        values = [value[k * rows : (k + 1) * rows] for k in range(inner)]
    else:
        values = [
            jnp.dot(ref[...], factors, preferred_element_type=jnp.float32) for ref in l_refs
        ]
    for k in range(inner):
        block = low ^ k
        owner = (block // per_col) ^ core
        at = pl.multiple_of((block % per_col) * rows, 8)
        for j in range(cols):

            @pl.when(owner == j)
            def _():
                out_refs[j][pl.ds(at, rows), :] = values[k]


def core_kernel(ids_ref, tiles_ref, *refs, inner, cols, width, first):
    bands_refs, s_refs = refs[:cols], refs[cols : cols + 2 * inner]
    out_refs, picked = refs[cols + 2 * inner : -1], refs[-1]
    high, low = ids_ref[0], ids_ref[1]
    per_col = bands_refs[0].shape[0]
    for j in range(cols):
        for b in range(per_col):
            source = slot_of(tiles_ref, bands_refs[j][b])
            block = low ^ (source % inner)
            slot = high ^ (source // inner)
            place = (j * per_col + b) * width
            for k in range(inner):

                @pl.when((block == k) & (slot < first))
                def _():
                    at = pl.multiple_of(slot * width, width)
                    picked[:, place : place + width] = s_refs[2 * k][:, pl.ds(at, width)]

                @pl.when((block == k) & (slot >= first))
                def _():
                    at = pl.multiple_of((slot - first) * width, width)
                    picked[:, place : place + width] = s_refs[2 * k + 1][:, pl.ds(at, width)]

    own = jnp.concatenate([s_refs[0][...], s_refs[1][...]], axis=1)
    value = cross_rows(own, picked[...])
    for j in range(cols):
        out_refs[j][...] = value[:, j * per_col * width : (j + 1) * per_col * width]


def split_kernel(*refs, outer):
    total = refs[0][...]
    for ref in refs[1:-outer]:
        total = total + ref[...]
    rows = total.shape[0] // outer
    for m in range(outer):
        refs[m - outer][...] = total[m * rows : (m + 1) * rows]


def round_kernel(*refs):
    total = refs[0][...]
    for ref in refs[1:-1]:
        total = total + ref[...]
    refs[-1][...] = total.astype(refs[-1].dtype)


def left_kernel(ids_ref, tiles_ref, ranks_ref, bands_ref, trail_ref, panel_ref, out_ref, *, width):
    own_tile = tiles_ref[ids_ref[3]]
    own_rank = ranks_ref[own_tile, own_tile]
    for b in range(bands_ref.shape[0]):
        stack = jnp.concatenate([trail_ref[0, b], panel_ref[0]], axis=1)
        mask = keep_mask(width, ranks_ref[own_tile, bands_ref[b]], own_rank)
        out_ref[0, b] = jnp.where(mask, cross_rows(stack, stack), 0.0)


def pick_kernel(ids_ref, tiles_ref, bands_ref, *refs, inner, outer):
    t_refs, out_refs = refs[:inner], refs[inner:]
    high, low = ids_ref[0], ids_ref[1]
    for b in range(bands_ref.shape[0]):
        block = low ^ (slot_of(tiles_ref, bands_ref[b]) % inner)
        for k in range(inner):

            @pl.when(block == k)
            def _():
                for m in range(outer):
                    out_refs[m][b] = t_refs[k][high ^ m]


def merge_kernel(ids_ref, tiles_ref, bands_ref, *refs, inner, outer):
    r_refs, out_ref = refs[:outer], refs[outer]
    high = ids_ref[0]
    for b in range(bands_ref.shape[0]):
        block = high ^ (slot_of(tiles_ref, bands_ref[b]) // inner)
        for m in range(outer):

            @pl.when(block == m)
            def _():
                out_ref[b] = r_refs[m][b]


def right_kernel(ids_ref, tiles_ref, ranks_ref, bands_ref, *refs, inner, outer, width):
    part_refs = refs[:outer]
    q_refs = refs[outer : outer + inner]
    trail_ref, out_ref, stack = refs[outer + inner :]
    high, low = ids_ref[0], ids_ref[1]
    own_tile = tiles_ref[ids_ref[3]]
    own_rank = ranks_ref[own_tile, own_tile]
    sub = q_refs[0].shape[2]
    rows = lax.broadcasted_iota(jnp.int32, (width, width), 0)
    cols = lax.broadcasted_iota(jnp.int32, (width, width), 1)
    for b in range(bands_ref.shape[0]):
        band_tile = bands_ref[b]
        lanes = slice(b * width, (b + 1) * width)
        total = part_refs[0][:, lanes]
        for m in range(1, outer):
            total = total + part_refs[m][:, lanes]
        live = (rows < own_rank) & (cols < ranks_ref[band_tile, band_tile])
        live = live & (band_tile < own_tile)
        core_mat = jnp.where(live, total, 0.0).astype(jnp.bfloat16)
        for p in range(inner * outer):
            stack[p, :, :width] = trail_ref[0, b, p]
        for k in range(inner):
            for m in range(outer):
                update = lax.dot_general(
                    q_refs[k][m, b],
                    core_mat,
                    (((1,), (1,)), ((), ())),
                    preferred_element_type=jnp.float32,
                )
                stack[(low ^ k) * outer + (high ^ m), :, width:] = -update.astype(jnp.bfloat16)
        if sub % 16 == 0:
            flat = stack[...].reshape(inner * outer * sub, 2 * width)
            gram = cross_rows(flat, flat)
        else:
            gram = jnp.zeros((2 * width, 2 * width), jnp.float32)
            for p in range(inner * outer):
                gram = gram + cross_rows(stack[p], stack[p])
        mask = keep_mask(width, ranks_ref[own_tile, band_tile], width)
        out_ref[0, b] = jnp.where(mask, gram, 0.0)


def call(kernel, outs, scalars, arrays, scratch=()):
    result = pl.pallas_call(
        kernel,
        out_shape=outs,
        in_specs=[SMEM] * len(scalars) + [VMEM] * len(arrays),
        out_specs=jax.tree.map(lambda _: VMEM, outs),
        scratch_shapes=scratch,
        compiler_params=pltpu.CompilerParams(vmem_limit_bytes=SCRATCH_BYTES),
    )(*scalars, *[pltpu.with_memory_space_constraint(x, pltpu.VMEM) for x in arrays])
    return list(result) if isinstance(outs, list) else result


def shards(panel_u, panel_v, linv, trail_u, trail_v, rank_map, tile_of_slot, band_cols, *, rows, cols):
    inner = 1
    while inner * inner < rows:
        inner *= 2
    outer = rows // inner
    points, width = panel_u.shape[1], panel_u.shape[2]
    per_col = band_cols.shape[0]
    sub = points // rows
    block_rows = linv.shape[0]
    kept_rows = inner // cols * block_rows
    f32, bf16 = jnp.float32, jnp.bfloat16
    row = lax.axis_index("row").astype(jnp.int32)
    core = lax.axis_index("col").astype(jnp.int32)
    high, low = row // inner, row % inner
    ids = jnp.stack([high, low, core, row])

    def swap(x, axis, distance, count):
        return lax.ppermute(x, axis, [(i, i ^ distance) for i in range(count)])

    def low_swap(x, k):
        return swap(x, "row", k, rows)

    def high_swap(x, m):
        return swap(x, "row", m * inner, rows)

    def core_swap(x, j):
        return swap(x, "col", j, cols)

    v_blocks = [panel_v[0]] + [None] * (outer - 1)
    for m in sorted(range(1, outer), key=lambda m: (m & (m - 1), -m)):
        low_bit = m & -m
        v_blocks[m] = lax.ppermute(
            v_blocks[m ^ low_bit], "row", [(r, r ^ (low_bit * inner)) for r in range(rows)]
        )
    if inner == 4:
        half = block_rows // 2
        first, second = linv[:half], linv[half:]
        y_first, x_second = low_swap(first, 2), low_swap(second, 1)
        x_first, y_second = low_swap(first, 1), low_swap(second, 2)
        far_first = lax.ppermute(y_first, "row", [(r, r ^ 1) for r in range(rows)])
        far_second = lax.ppermute(x_second, "row", [(r, r ^ 2) for r in range(rows)])
        l_blocks = [linv, x_first, x_second, y_first, y_second, far_first, far_second]
        pieces = (1, 2, 2, 2)
    else:
        l_blocks = [linv] + [low_swap(linv, k) for k in range(1, inner)]
        pieces = (1,) * inner
    bands = [band_cols] + [core_swap(band_cols, j) for j in range(1, cols)]

    gram_left = call(
        functools.partial(left_kernel, width=width),
        jax.ShapeDtypeStruct((1, per_col, 2 * width, 2 * width), f32),
        (ids, tile_of_slot, rank_map, band_cols),
        (trail_u, panel_u),
    )

    chunks = panel_u[0].reshape(inner, outer, sub, width)
    t_blocks = [
        lax.dynamic_index_in_dim(chunks, low ^ k, 0, keepdims=False) for k in range(inner)
    ]
    t_blocks = t_blocks[:1] + [low_swap(t_blocks[k], k) for k in range(1, inner)]
    small = pltpu.VMEM((per_col, sub, width), bf16)
    sends = call(
        functools.partial(pick_kernel, inner=inner, outer=outer),
        [small] * outer,
        (ids, tile_of_slot, band_cols),
        t_blocks,
    )
    got = sends[:1] + [high_swap(sends[m], m) for m in range(1, outer)]
    piece = call(
        functools.partial(merge_kernel, inner=inner, outer=outer),
        small,
        (ids, tile_of_slot, band_cols),
        got,
    )
    bases = jnp.stack([piece] + [high_swap(piece, m) for m in range(1, outer)])
    base_blocks = [bases] + [low_swap(bases, k) for k in range(1, inner)]

    early = outer - 1
    solved_blocks = []
    for slots in (v_blocks[:early], v_blocks[early:]):
        lanes = len(slots) * width
        parts = call(
            functools.partial(solve_kernel, pieces=pieces, cols=cols),
            [pltpu.VMEM((kept_rows, lanes), f32)] * cols,
            (ids,),
            (*l_blocks, *slots),
        )
        solved = call(
            round_kernel,
            pltpu.VMEM((kept_rows, lanes), bf16),
            (),
            parts[:1] + [core_swap(parts[j], j) for j in range(1, cols)],
        )
        solved_blocks.append([solved] + [low_swap(solved, k) for k in range(1, inner)])
    cores = call(
        functools.partial(core_kernel, inner=inner, cols=cols, width=width, first=early),
        [pltpu.VMEM((outer * width, per_col * width), f32)] * cols,
        (ids, tile_of_slot, *bands),
        [block for pair in zip(*solved_blocks) for block in pair],
        [pltpu.VMEM((kept_rows, cols * per_col * width), bf16)],
    )
    core_parts = call(
        functools.partial(split_kernel, outer=outer),
        [pltpu.VMEM((width, per_col * width), f32)] * outer,
        (),
        cores[:1] + [core_swap(cores[j], j) for j in range(1, cols)],
    )
    core_parts = core_parts[:1] + [high_swap(core_parts[m], m) for m in range(1, outer)]

    gram_right = call(
        functools.partial(right_kernel, inner=inner, outer=outer, width=width),
        jax.ShapeDtypeStruct((1, per_col, 2 * width, 2 * width), f32),
        (ids, tile_of_slot, rank_map, band_cols),
        (*core_parts, *base_blocks, trail_v.reshape(1, per_col, inner * outer, sub, width)),
        [pltpu.VMEM((inner * outer, sub, 2 * width), bf16)],
    )
    return gram_left, gram_right


def solution(mesh):
    rows, cols = mesh.shape["row"], mesh.shape["col"]

    def body(*args):
        return shards(*args, rows=rows, cols=cols)

    return jax.shard_map(
        body,
        mesh=mesh,
        in_specs=(
            P("row", None, None),
            P("row", "col", None),
            P("row", "col"),
            P("row", "col", None, None),
            P("row", "col", None, None),
            P(),
            P(),
            P("col"),
        ),
        out_specs=(P("row", "col", None, None), P("row", "col", None, None)),
        check_vma=False,
    )
```

```python
import functools

import jax
import jax.numpy as jnp
from jax import lax
from jax.experimental import pallas as pl
from jax.experimental.pallas import tpu as pltpu
from jax.sharding import PartitionSpec as P


SCRATCH_BYTES = 16 * 1024 * 1024

VMEM = pl.BlockSpec(memory_space=pltpu.VMEM)
SMEM = pl.BlockSpec(memory_space=pltpu.SMEM)


def cross_rows(first, second):
    return lax.dot_general(
        first, second, (((0,), (0,)), ((), ())), preferred_element_type=jnp.float32
    )


def slot_of(tiles_ref, tile):
    slot = jnp.int32(0)
    for s in range(tiles_ref.shape[0]):
        slot = jnp.where(tiles_ref[s] == tile, jnp.int32(s), slot)
    return slot


def keep_mask(width, first_rank, second_rank):
    rows = lax.broadcasted_iota(jnp.int32, (2 * width, 2 * width), 0)
    cols = lax.broadcasted_iota(jnp.int32, (2 * width, 2 * width), 1)

    def kept(ids):
        return ids < jnp.where(ids < width, first_rank, second_rank + width)

    return kept(rows) & kept(cols)


def solve_kernel(ids_ref, *refs, pieces, cols):
    inner = len(pieces)
    count = sum(pieces)
    l_refs, v_refs, out_refs = refs[:count], refs[count : len(refs) - cols], refs[-cols:]
    per_col = inner // cols
    low, core = ids_ref[1], ids_ref[2]
    factors = jnp.concatenate([ref[...] for ref in v_refs], axis=1)
    rows = l_refs[0].shape[0]
    if rows % 16 == 0:
        lines = jnp.concatenate([ref[...] for ref in l_refs], axis=0)
        value = jnp.dot(lines, factors, preferred_element_type=jnp.float32)
        values = [value[k * rows : (k + 1) * rows] for k in range(inner)]
    else:
        values = [
            jnp.dot(ref[...], factors, preferred_element_type=jnp.float32) for ref in l_refs
        ]
    for k in range(inner):
        block = low ^ k
        owner = (block // per_col) ^ core
        at = pl.multiple_of((block % per_col) * rows, 8)
        for j in range(cols):

            @pl.when(owner == j)
            def _():
                out_refs[j][pl.ds(at, rows), :] = values[k]


def core_kernel(ids_ref, tiles_ref, *refs, inner, cols, width, first):
    bands_refs, s_refs = refs[:cols], refs[cols : cols + 2 * inner]
    out_refs, picked = refs[cols + 2 * inner : -1], refs[-1]
    high, low = ids_ref[0], ids_ref[1]
    per_col = bands_refs[0].shape[0]
    for j in range(cols):
        for b in range(per_col):
            source = slot_of(tiles_ref, bands_refs[j][b])
            block = low ^ (source % inner)
            slot = high ^ (source // inner)
            place = (j * per_col + b) * width
            for k in range(inner):

                @pl.when((block == k) & (slot < first))
                def _():
                    at = pl.multiple_of(slot * width, width)
                    picked[:, place : place + width] = s_refs[2 * k][:, pl.ds(at, width)]

                @pl.when((block == k) & (slot >= first))
                def _():
                    at = pl.multiple_of((slot - first) * width, width)
                    picked[:, place : place + width] = s_refs[2 * k + 1][:, pl.ds(at, width)]

    own = jnp.concatenate([s_refs[0][...], s_refs[1][...]], axis=1)
    value = cross_rows(own, picked[...])
    for j in range(cols):
        out_refs[j][...] = value[:, j * per_col * width : (j + 1) * per_col * width]


def split_kernel(*refs, outer):
    total = refs[0][...]
    for ref in refs[1:-outer]:
        total = total + ref[...]
    rows = total.shape[0] // outer
    for m in range(outer):
        refs[m - outer][...] = total[m * rows : (m + 1) * rows]


def round_kernel(*refs):
    total = refs[0][...]
    for ref in refs[1:-1]:
        total = total + ref[...]
    refs[-1][...] = total.astype(refs[-1].dtype)


def left_kernel(ids_ref, tiles_ref, ranks_ref, bands_ref, trail_ref, panel_ref, out_ref, *, width):
    own_tile = tiles_ref[ids_ref[3]]
    own_rank = ranks_ref[own_tile, own_tile]
    for b in range(bands_ref.shape[0]):
        stack = jnp.concatenate([trail_ref[0, b], panel_ref[0]], axis=1)
        mask = keep_mask(width, ranks_ref[own_tile, bands_ref[b]], own_rank)
        out_ref[0, b] = jnp.where(mask, cross_rows(stack, stack), 0.0)


def pick_kernel(ids_ref, tiles_ref, *refs, inner, share):
    bands_refs, t_refs, out_refs = refs[:share], refs[share : share + inner], refs[share + inner :]
    for j in range(share):
        for b in range(bands_refs[j].shape[0]):
            block = ids_ref[1] ^ (slot_of(tiles_ref, bands_refs[j][b]) % inner)
            for k in range(inner):

                @pl.when(block == k)
                def _():
                    out_refs[j][b] = t_refs[k][...]


def join_kernel(*refs):
    size = refs[0].shape[1]
    for j, ref in enumerate(refs[:-1]):
        refs[-1][:, j * size : (j + 1) * size] = ref[...]


def halves_kernel(y_ref, x_ref, first_ref, second_ref):
    half = first_ref.shape[1]
    first_ref[...] = y_ref[:, :half]
    second_ref[...] = x_ref[:, half:]


def merge_kernel(ids_ref, tiles_ref, bands_ref, kept_ref, got_ref, out_ref, *, inner, bit):
    for b in range(bands_ref.shape[0]):
        other = ((slot_of(tiles_ref, bands_ref[b]) // inner) ^ ids_ref[0]) & bit

        @pl.when(other == 0)
        def _():
            out_ref[b] = kept_ref[b]

        @pl.when(other != 0)
        def _():
            out_ref[b] = got_ref[b]


def right_kernel(
    ids_ref, tiles_ref, ranks_ref, bands_ref, *refs, pieces, outer, width, share
):
    part_refs = refs[:outer]
    q_refs = refs[outer : outer + sum(pieces)]
    trail_ref, out_ref, stack = refs[outer + sum(pieces) :]
    low, core = ids_ref[1], ids_ref[2] if share > 1 else 0
    own_tile = tiles_ref[ids_ref[3]]
    own_rank = ranks_ref[own_tile, own_tile]
    quarter = stack.shape[0] // len(pieces)
    rows = lax.broadcasted_iota(jnp.int32, (width, width), 0)
    cols = lax.broadcasted_iota(jnp.int32, (width, width), 1)
    for b in range(bands_ref.shape[0]):
        band_tile = bands_ref[b]
        lanes = slice(b * width, (b + 1) * width)
        total = part_refs[0][:, lanes]
        for m in range(1, outer):
            total = total + part_refs[m][:, lanes]
        live = (rows < own_rank) & (cols < ranks_ref[band_tile, band_tile])
        live = live & (band_tile < own_tile)
        core_mat = jnp.where(live, total, 0.0).astype(jnp.bfloat16)
        stack[:, :width] = trail_ref[0, b]
        at = 0
        for k, count in enumerate(pieces):
            blocks = max(share, count)
            size = quarter // blocks
            for h in range(blocks):
                part, j = h * count // blocks, h * share // blocks
                update = lax.dot_general(
                    q_refs[at + part][b, pl.ds((h - part * blocks // count) * size, size), :],
                    core_mat,
                    (((1,), (1,)), ((), ())),
                    preferred_element_type=jnp.float32,
                )
                inside = (core ^ j) * (quarter // share) + (h - j * blocks // share) * size
                place = pl.multiple_of((low ^ k) * quarter + inside, 16)
                stack[pl.ds(place, size), width:] = -update.astype(jnp.bfloat16)
            at += count
        gram = cross_rows(stack[...], stack[...])
        mask = keep_mask(width, ranks_ref[own_tile, band_tile], width)
        out_ref[0, b] = jnp.where(mask, gram, 0.0)


def call(kernel, outs, scalars, arrays, scratch=()):
    result = pl.pallas_call(
        kernel,
        out_shape=outs,
        in_specs=[SMEM] * len(scalars) + [VMEM] * len(arrays),
        out_specs=jax.tree.map(lambda _: VMEM, outs),
        scratch_shapes=scratch,
        compiler_params=pltpu.CompilerParams(vmem_limit_bytes=SCRATCH_BYTES),
    )(*scalars, *[pltpu.with_memory_space_constraint(x, pltpu.VMEM) for x in arrays])
    return list(result) if isinstance(outs, list) else result


def shards(panel_u, panel_v, linv, trail_u, trail_v, rank_map, tile_of_slot, band_cols, *, rows, cols):
    inner = 1
    while inner * inner < rows:
        inner *= 2
    outer = rows // inner
    points, width = panel_u.shape[1], panel_u.shape[2]
    per_col = band_cols.shape[0]
    block_rows = linv.shape[0]
    kept_rows = inner // cols * block_rows
    f32, bf16 = jnp.float32, jnp.bfloat16
    row = lax.axis_index("row").astype(jnp.int32)
    core = lax.axis_index("col").astype(jnp.int32)
    high, low = row // inner, row % inner
    ids = jnp.stack([high, low, core, row])

    def swap(x, axis, distance, count):
        return lax.ppermute(x, axis, [(i, i ^ distance) for i in range(count)])

    def low_swap(x, k):
        return swap(x, "row", k, rows)

    def high_swap(x, m):
        return swap(x, "row", m * inner, rows)

    def core_swap(x, j):
        return swap(x, "col", j, cols)

    v_blocks = [panel_v[0]] + [None] * (outer - 1)
    for m in sorted(range(1, outer), key=lambda m: (m & (m - 1), -m)):
        low_bit = m & -m
        v_blocks[m] = lax.ppermute(
            v_blocks[m ^ low_bit], "row", [(r, r ^ (low_bit * inner)) for r in range(rows)]
        )
    if inner == 4:
        half = block_rows // 2
        x_block, y_block = low_swap(linv, 1), low_swap(linv, 2)
        far_first = lax.ppermute(y_block[:half], "row", [(r, r ^ 1) for r in range(rows)])
        far_second = lax.ppermute(x_block[half:], "row", [(r, r ^ 2) for r in range(rows)])
        l_blocks = [linv, x_block, y_block, far_first, far_second]
        pieces = (1, 1, 1, 2)
    else:
        l_blocks = [linv] + [low_swap(linv, k) for k in range(1, inner)]
        pieces = (1,) * inner
    bands = [band_cols] + [core_swap(band_cols, j) for j in range(1, cols)]

    gram_left = call(
        functools.partial(left_kernel, width=width),
        jax.ShapeDtypeStruct((1, per_col, 2 * width, 2 * width), f32),
        (ids, tile_of_slot, rank_map, band_cols),
        (trail_u, panel_u),
    )

    quarter = points // inner
    share = cols if quarter % (cols * 16) == 0 else 1
    size = quarter // share
    mine = core * size if share > 1 else 0
    t_blocks = [
        lax.dynamic_slice_in_dim(panel_u[0], (low ^ k) * quarter + mine, size)
        for k in range(inner)
    ]
    t_blocks = t_blocks[:1] + [low_swap(t_blocks[k], k) for k in range(1, inner)]
    picked = call(
        functools.partial(pick_kernel, inner=inner, share=share),
        [pltpu.VMEM((per_col, size, width), bf16)] * share,
        (ids, tile_of_slot, *bands[:share]),
        t_blocks,
    )
    base = picked[0]
    if share > 1:
        base = call(
            join_kernel,
            pltpu.VMEM((per_col, quarter, width), bf16),
            (),
            picked[:1] + [core_swap(picked[j], j) for j in range(1, share)],
        )
    bit = outer // 2
    while bit:
        base = call(
            functools.partial(merge_kernel, inner=inner, bit=bit),
            pltpu.VMEM((per_col, quarter, width), bf16),
            (ids, tile_of_slot, band_cols),
            (base, high_swap(base, bit)),
        )
        bit //= 2
    base_blocks = [base] + [low_swap(base, k) for k in range(1, 3 if inner == 4 else inner)]
    base_pieces = (1,) * inner
    if inner == 4:
        far = call(
            halves_kernel,
            [pltpu.VMEM((per_col, quarter // 2, width), bf16)] * 2,
            (),
            (base_blocks[2], base_blocks[1]),
        )
        base_blocks += [swap(far[0], "row", 1, rows), swap(far[1], "row", 2, rows)]
        base_pieces = (1, 1, 1, 2)

    early = outer - 1
    solved_blocks = []
    for slots in (v_blocks[:early], v_blocks[early:]):
        lanes = len(slots) * width
        parts = call(
            functools.partial(solve_kernel, pieces=pieces, cols=cols),
            [pltpu.VMEM((kept_rows, lanes), f32)] * cols,
            (ids,),
            (*l_blocks, *slots),
        )
        solved = call(
            round_kernel,
            pltpu.VMEM((kept_rows, lanes), bf16),
            (),
            parts[:1] + [core_swap(parts[j], j) for j in range(1, cols)],
        )
        solved_blocks.append([solved] + [low_swap(solved, k) for k in range(1, inner)])
    cores = call(
        functools.partial(core_kernel, inner=inner, cols=cols, width=width, first=early),
        [pltpu.VMEM((outer * width, per_col * width), f32)] * cols,
        (ids, tile_of_slot, *bands),
        [block for pair in zip(*solved_blocks) for block in pair],
        [pltpu.VMEM((kept_rows, cols * per_col * width), bf16)],
    )
    core_parts = call(
        functools.partial(split_kernel, outer=outer),
        [pltpu.VMEM((width, per_col * width), f32)] * outer,
        (),
        cores[:1] + [core_swap(cores[j], j) for j in range(1, cols)],
    )
    core_parts = core_parts[:1] + [high_swap(core_parts[m], m) for m in range(1, outer)]

    gram_right = call(
        functools.partial(right_kernel, pieces=base_pieces, outer=outer, width=width, share=share),
        jax.ShapeDtypeStruct((1, per_col, 2 * width, 2 * width), f32),
        (ids, tile_of_slot, rank_map, band_cols),
        (*core_parts, *base_blocks, trail_v),
        [pltpu.VMEM((points, 2 * width), bf16)],
    )
    return gram_left, gram_right


def solution(mesh):
    rows, cols = mesh.shape["row"], mesh.shape["col"]

    def body(*args):
        return shards(*args, rows=rows, cols=cols)

    return jax.shard_map(
        body,
        mesh=mesh,
        in_specs=(
            P("row", None, None),
            P("row", "col", None),
            P("row", "col"),
            P("row", "col", None, None),
            P("row", "col", None, None),
            P(),
            P(),
            P("col"),
        ),
        out_specs=(P("row", "col", None, None), P("row", "col", None, None)),
        check_vma=False,
    )
```

```python
import functools

import jax
import jax.numpy as jnp
from jax import lax
from jax.experimental import pallas as pl
from jax.experimental.pallas import tpu as pltpu
from jax.sharding import PartitionSpec as P


SCRATCH_BYTES = 16 * 1024 * 1024

VMEM = pl.BlockSpec(memory_space=pltpu.VMEM)
SMEM = pl.BlockSpec(memory_space=pltpu.SMEM)


def cross_rows(first, second):
    return lax.dot_general(
        first, second, (((0,), (0,)), ((), ())), preferred_element_type=jnp.float32
    )


def slot_of(tiles_ref, tile):
    slot = jnp.int32(0)
    for s in range(tiles_ref.shape[0]):
        slot = jnp.where(tiles_ref[s] == tile, jnp.int32(s), slot)
    return slot


def keep_mask(width, first_rank, second_rank):
    rows = lax.broadcasted_iota(jnp.int32, (2 * width, 2 * width), 0)
    cols = lax.broadcasted_iota(jnp.int32, (2 * width, 2 * width), 1)

    def kept(ids):
        return ids < jnp.where(ids < width, first_rank, second_rank + width)

    return kept(rows) & kept(cols)


def solve_kernel(ids_ref, *refs, pieces, cols):
    inner = len(pieces)
    count = sum(pieces)
    l_refs, v_refs, out_refs = refs[:count], refs[count : len(refs) - cols], refs[-cols:]
    per_col = inner // cols
    low, core = ids_ref[1], ids_ref[2]
    factors = jnp.concatenate([ref[...] for ref in v_refs], axis=1)
    rows = l_refs[0].shape[0]
    if rows % 16 == 0:
        lines = jnp.concatenate([ref[...] for ref in l_refs], axis=0)
        value = jnp.dot(lines, factors, preferred_element_type=jnp.float32)
        values = [value[k * rows : (k + 1) * rows] for k in range(inner)]
    else:
        values = [
            jnp.dot(ref[...], factors, preferred_element_type=jnp.float32) for ref in l_refs
        ]
    for k in range(inner):
        block = low ^ k
        owner = (block // per_col) ^ core
        at = pl.multiple_of((block % per_col) * rows, 8)
        for j in range(cols):

            @pl.when(owner == j)
            def _():
                out_refs[j][pl.ds(at, rows), :] = values[k]


def core_kernel(ids_ref, tiles_ref, *refs, inner, cols, width, first):
    bands_refs, s_refs = refs[:cols], refs[cols : cols + 2 * inner]
    out_refs, picked = refs[cols + 2 * inner : -1], refs[-1]
    high, low = ids_ref[0], ids_ref[1]
    per_col = bands_refs[0].shape[0]
    for j in range(cols):
        for b in range(per_col):
            source = slot_of(tiles_ref, bands_refs[j][b])
            block = low ^ (source % inner)
            slot = high ^ (source // inner)
            place = (j * per_col + b) * width
            for k in range(inner):

                @pl.when((block == k) & (slot < first))
                def _():
                    at = pl.multiple_of(slot * width, width)
                    picked[:, place : place + width] = s_refs[2 * k][:, pl.ds(at, width)]

                @pl.when((block == k) & (slot >= first))
                def _():
                    at = pl.multiple_of((slot - first) * width, width)
                    picked[:, place : place + width] = s_refs[2 * k + 1][:, pl.ds(at, width)]

    own = jnp.concatenate([s_refs[0][...], s_refs[1][...]], axis=1)
    value = cross_rows(own, picked[...])
    for j in range(cols):
        out_refs[j][...] = value[:, j * per_col * width : (j + 1) * per_col * width]


def split_kernel(*refs, outer):
    total = refs[0][...]
    for ref in refs[1:-outer]:
        total = total + ref[...]
    rows = total.shape[0] // outer
    for m in range(outer):
        refs[m - outer][...] = total[m * rows : (m + 1) * rows]


def round_kernel(*refs):
    total = refs[0][...]
    for ref in refs[1:-1]:
        total = total + ref[...]
    refs[-1][...] = total.astype(refs[-1].dtype)


def left_kernel(
    ids_ref, tiles_ref, ranks_ref, bands_ref, trail_ref, panel_ref, right_ref, out_ref, kept_ref, *, width
):
    own_tile = tiles_ref[ids_ref[3]]
    own_rank = ranks_ref[own_tile, own_tile]
    for b in range(bands_ref.shape[0]):
        stack = jnp.concatenate([trail_ref[0, b], panel_ref[0]], axis=1)
        mask = keep_mask(width, ranks_ref[own_tile, bands_ref[b]], own_rank)
        out_ref[0, b] = jnp.where(mask, cross_rows(stack, stack), 0.0)
        kept_ref[b] = jnp.where(
            mask[:width, :width], cross_rows(right_ref[0, b], right_ref[0, b]), 0.0
        )


def pick_kernel(ids_ref, tiles_ref, *refs, inner, share):
    bands_refs, t_refs, out_refs = refs[:share], refs[share : share + inner], refs[share + inner :]
    for j in range(share):
        for b in range(bands_refs[j].shape[0]):
            block = ids_ref[1] ^ (slot_of(tiles_ref, bands_refs[j][b]) % inner)
            for k in range(inner):

                @pl.when(block == k)
                def _():
                    out_refs[j][b] = t_refs[k][...]


def join_kernel(*refs):
    size = refs[0].shape[1]
    for j, ref in enumerate(refs[:-1]):
        refs[-1][:, j * size : (j + 1) * size] = ref[...]


def sort_kernel(ids_ref, own_ref, other_ref, kept_ref, sent_ref):
    same = (ids_ref[2] ^ ids_ref[4]) == 0

    @pl.when(same)
    def _():
        kept_ref[...] = own_ref[...]
        sent_ref[...] = other_ref[...]

    @pl.when(jnp.logical_not(same))
    def _():
        kept_ref[...] = other_ref[...]
        sent_ref[...] = own_ref[...]


def merge_kernel(ids_ref, tiles_ref, bands_ref, kept_ref, got_ref, out_ref, *, inner, bit):
    for b in range(bands_ref.shape[0]):
        other = ((slot_of(tiles_ref, bands_ref[b]) // inner) ^ ids_ref[0]) & bit

        @pl.when(other == 0)
        def _():
            out_ref[b] = kept_ref[b]

        @pl.when(other != 0)
        def _():
            out_ref[b] = got_ref[b]


def right_kernel(
    ids_ref, tiles_ref, ranks_ref, bands_ref, *refs, pieces, outer, width, share
):
    part_refs = refs[:outer]
    q_refs = refs[outer : outer + sum(pieces)]
    kept_ref, trail_ref, out_ref, stack = refs[outer + sum(pieces) :]
    low, flip = ids_ref[1], ids_ref[4] if share > 1 else 0
    own_tile = tiles_ref[ids_ref[3]]
    own_rank = ranks_ref[own_tile, own_tile]
    quarter = stack.shape[0] // len(pieces)
    rows = lax.broadcasted_iota(jnp.int32, (width, width), 0)
    cols = lax.broadcasted_iota(jnp.int32, (width, width), 1)
    for b in range(bands_ref.shape[0]):
        band_tile = bands_ref[b]
        lanes = slice(b * width, (b + 1) * width)
        total = part_refs[0][:, lanes]
        for m in range(1, outer):
            total = total + part_refs[m][:, lanes]
        live = (rows < own_rank) & (cols < ranks_ref[band_tile, band_tile])
        live = live & (band_tile < own_tile)
        core_mat = jnp.where(live, total, 0.0).astype(jnp.bfloat16)
        at = 0
        for k, count in enumerate(pieces):
            blocks = max(share, count)
            size = quarter // blocks
            for h in range(blocks):
                part, j = h * count // blocks, h * share // blocks
                update = lax.dot_general(
                    q_refs[at + part][b, pl.ds((h - part * blocks // count) * size, size), :],
                    core_mat,
                    (((1,), (1,)), ((), ())),
                    preferred_element_type=jnp.float32,
                )
                inside = (flip ^ j) * (quarter // share) + (h - j * blocks // share) * size
                place = pl.multiple_of((low ^ k) * quarter + inside, 16)
                stack[pl.ds(place, size), :] = -update.astype(jnp.bfloat16)
            at += count
        change = stack[...]
        both = cross_rows(change, jnp.concatenate([trail_ref[0, b], change], axis=1))
        rank = ranks_ref[own_tile, band_tile]
        mixed = jnp.where(cols < rank, both[:, :width], 0.0)
        out_ref[0, b, :width, :width] = kept_ref[b]
        out_ref[0, b, :width, width:] = mixed.T
        out_ref[0, b, width:, :width] = mixed
        out_ref[0, b, width:, width:] = both[:, width:]


def call(kernel, outs, scalars, arrays, scratch=()):
    result = pl.pallas_call(
        kernel,
        out_shape=outs,
        in_specs=[SMEM] * len(scalars) + [VMEM] * len(arrays),
        out_specs=jax.tree.map(lambda _: VMEM, outs),
        scratch_shapes=scratch,
        compiler_params=pltpu.CompilerParams(vmem_limit_bytes=SCRATCH_BYTES),
    )(*scalars, *[pltpu.with_memory_space_constraint(x, pltpu.VMEM) for x in arrays])
    return list(result) if isinstance(outs, list) else result


def shards(panel_u, panel_v, linv, trail_u, trail_v, rank_map, tile_of_slot, band_cols, *, rows, cols):
    inner = 1
    while inner * inner < rows:
        inner *= 2
    outer = rows // inner
    points, width = panel_u.shape[1], panel_u.shape[2]
    per_col = band_cols.shape[0]
    block_rows = linv.shape[0]
    kept_rows = inner // cols * block_rows
    f32, bf16 = jnp.float32, jnp.bfloat16
    row = lax.axis_index("row").astype(jnp.int32)
    core = lax.axis_index("col").astype(jnp.int32)
    high, low = row // inner, row % inner
    halved = inner == 4 and outer == 4 and cols == 2
    ids = jnp.stack([high, low, core, row, high % 2 if halved else core])

    def swap(x, axis, distance, count):
        return lax.ppermute(x, axis, [(i, i ^ distance) for i in range(count)])

    def low_swap(x, k):
        return swap(x, "row", k, rows)

    def high_swap(x, m):
        return swap(x, "row", m * inner, rows)

    def core_swap(x, j):
        return swap(x, "col", j, cols)

    v_blocks = [panel_v[0]] + [None] * (outer - 1)
    for m in sorted(range(1, outer), key=lambda m: (m & (m - 1), -m)):
        low_bit = m & -m
        v_blocks[m] = lax.ppermute(
            v_blocks[m ^ low_bit], "row", [(r, r ^ (low_bit * inner)) for r in range(rows)]
        )
    if inner == 4:
        half = block_rows // 2
        x_block, y_block = low_swap(linv, 1), low_swap(linv, 2)
        far_first = lax.ppermute(y_block[:half], "row", [(r, r ^ 1) for r in range(rows)])
        far_second = lax.ppermute(x_block[half:], "row", [(r, r ^ 2) for r in range(rows)])
        l_blocks = [linv, x_block, y_block, far_first, far_second]
        pieces = (1, 1, 1, 2)
    else:
        l_blocks = [linv] + [low_swap(linv, k) for k in range(1, inner)]
        pieces = (1,) * inner
    bands = [band_cols] + [core_swap(band_cols, j) for j in range(1, cols)]

    gram_left, gram_kept = call(
        functools.partial(left_kernel, width=width),
        [
            jax.ShapeDtypeStruct((1, per_col, 2 * width, 2 * width), f32),
            pltpu.VMEM((per_col, width, width), f32),
        ],
        (ids, tile_of_slot, rank_map, band_cols),
        (trail_u, panel_u, trail_v),
    )

    quarter = points // inner
    share = cols if quarter % (cols * 16) == 0 else 1
    size = quarter // share
    split_rows = halved and share == 2
    mine = core * size if share > 1 else 0
    t_blocks = [
        lax.dynamic_slice_in_dim(panel_u[0], (low ^ k) * quarter + mine, size)
        for k in range(inner)
    ]
    t_blocks = t_blocks[:1] + [low_swap(t_blocks[k], k) for k in range(1, inner)]
    picked = call(
        functools.partial(pick_kernel, inner=inner, share=share),
        [pltpu.VMEM((per_col, size, width), bf16)] * share,
        (ids, tile_of_slot, *bands[:share]),
        t_blocks,
    )

    def merged(kept, got, bit):
        return call(
            functools.partial(merge_kernel, inner=inner, bit=bit),
            pltpu.VMEM(kept.shape, bf16),
            (ids, tile_of_slot, band_cols),
            (kept, got),
        )

    base = picked[0]
    exchanged = picked[:1] + [core_swap(picked[j], j) for j in range(1, share)]
    if split_rows:
        kept, sent = call(
            sort_kernel, [pltpu.VMEM((per_col, size, width), bf16)] * 2, (ids,), exchanged
        )
        kept = merged(kept, high_swap(sent, 1), 1)
        kept = merged(kept, high_swap(kept, 2), 2)
        rest = high_swap(kept, 1)
        kept_y, rest_x = low_swap(kept, 2), low_swap(rest, 1)
        kept_x, rest_y = low_swap(kept, 1), low_swap(rest, 2)
        far = [swap(kept_y, "row", 1, rows), swap(rest_x, "row", 2, rows)]
        base_blocks = [kept, rest, kept_x, rest_x, kept_y, rest_y, *far]
        base_pieces = (2,) * inner
    else:
        if share > 1:
            base = call(join_kernel, pltpu.VMEM((per_col, quarter, width), bf16), (), exchanged)
        bit = outer // 2
        while bit:
            base = merged(base, high_swap(base, bit), bit)
            bit //= 2
        base_blocks = [base] + [low_swap(base, k) for k in range(1, inner)]
        base_pieces = (1,) * inner

    early = outer - 1
    solved_blocks = []
    for slots in (v_blocks[:early], v_blocks[early:]):
        lanes = len(slots) * width
        parts = call(
            functools.partial(solve_kernel, pieces=pieces, cols=cols),
            [pltpu.VMEM((kept_rows, lanes), f32)] * cols,
            (ids,),
            (*l_blocks, *slots),
        )
        solved = call(
            round_kernel,
            pltpu.VMEM((kept_rows, lanes), bf16),
            (),
            parts[:1] + [core_swap(parts[j], j) for j in range(1, cols)],
        )
        solved_blocks.append([solved] + [low_swap(solved, k) for k in range(1, inner)])
    cores = call(
        functools.partial(core_kernel, inner=inner, cols=cols, width=width, first=early),
        [pltpu.VMEM((outer * width, per_col * width), f32)] * cols,
        (ids, tile_of_slot, *bands),
        [block for pair in zip(*solved_blocks) for block in pair],
        [pltpu.VMEM((kept_rows, cols * per_col * width), bf16)],
    )
    core_parts = call(
        functools.partial(split_kernel, outer=outer),
        [pltpu.VMEM((width, per_col * width), f32)] * outer,
        (),
        cores[:1] + [core_swap(cores[j], j) for j in range(1, cols)],
    )
    core_parts = core_parts[:1] + [high_swap(core_parts[m], m) for m in range(1, outer)]

    gram_right = call(
        functools.partial(right_kernel, pieces=base_pieces, outer=outer, width=width, share=share),
        jax.ShapeDtypeStruct((1, per_col, 2 * width, 2 * width), f32),
        (ids, tile_of_slot, rank_map, band_cols),
        (*core_parts, *base_blocks, gram_kept, trail_v),
        [pltpu.VMEM((points, width), bf16)],
    )
    return gram_left, gram_right


def solution(mesh):
    rows, cols = mesh.shape["row"], mesh.shape["col"]

    def body(*args):
        return shards(*args, rows=rows, cols=cols)

    return jax.shard_map(
        body,
        mesh=mesh,
        in_specs=(
            P("row", None, None),
            P("row", "col", None),
            P("row", "col"),
            P("row", "col", None, None),
            P("row", "col", None, None),
            P(),
            P(),
            P("col"),
        ),
        out_specs=(P("row", "col", None, None), P("row", "col", None, None)),
        check_vma=False,
    )
```

```python
import functools

import jax
import jax.numpy as jnp
from jax import lax
from jax.experimental import pallas as pl
from jax.experimental.pallas import tpu as pltpu
from jax.sharding import PartitionSpec as P


SCRATCH_BYTES = 16 * 1024 * 1024

VMEM = pl.BlockSpec(memory_space=pltpu.VMEM)
SMEM = pl.BlockSpec(memory_space=pltpu.SMEM)


def cross_rows(first, second):
    return lax.dot_general(
        first, second, (((0,), (0,)), ((), ())), preferred_element_type=jnp.float32
    )


def slot_of(tiles_ref, tile):
    slot = jnp.int32(0)
    for s in range(tiles_ref.shape[0]):
        slot = jnp.where(tiles_ref[s] == tile, jnp.int32(s), slot)
    return slot


def keep_mask(width, first_rank, second_rank):
    rows = lax.broadcasted_iota(jnp.int32, (2 * width, 2 * width), 0)
    cols = lax.broadcasted_iota(jnp.int32, (2 * width, 2 * width), 1)

    def kept(ids):
        return ids < jnp.where(ids < width, first_rank, second_rank + width)

    return kept(rows) & kept(cols)


def table_kernel(tiles_ref, *refs):
    at = 0
    for bands_ref in refs[:-1]:
        for b in range(bands_ref.shape[0]):
            refs[-1][at] = slot_of(tiles_ref, bands_ref[b])
            at += 1


def solve_kernel(ids_ref, *refs, pieces, cols):
    inner = len(pieces)
    count = sum(pieces)
    l_refs, v_refs, out_refs = refs[:count], refs[count : len(refs) - cols], refs[-cols:]
    per_col = inner // cols
    low, core = ids_ref[1], ids_ref[2]
    factors = jnp.concatenate([ref[...] for ref in v_refs], axis=1)
    rows = l_refs[0].shape[0]
    if rows % 16 == 0:
        lines = jnp.concatenate([ref[...] for ref in l_refs], axis=0)
        value = jnp.dot(lines, factors, preferred_element_type=jnp.float32)
        values = [value[k * rows : (k + 1) * rows] for k in range(inner)]
    else:
        values = [
            jnp.dot(ref[...], factors, preferred_element_type=jnp.float32) for ref in l_refs
        ]
    for k in range(inner):
        block = low ^ k
        owner = (block // per_col) ^ core
        at = pl.multiple_of((block % per_col) * rows, 8)
        for j in range(cols):

            @pl.when(owner == j)
            def _():
                out_refs[j][pl.ds(at, rows), :] = values[k]


def core_kernel(ids_ref, sources_ref, *refs, inner, cols, width, first):
    bands_refs, s_refs = refs[:cols], refs[cols : cols + 2 * inner]
    out_refs, picked = refs[cols + 2 * inner : -1], refs[-1]
    high, low = ids_ref[0], ids_ref[1]
    per_col = bands_refs[0].shape[0]
    for j in range(cols):
        for b in range(per_col):
            source = sources_ref[j * per_col + b]
            block = low ^ (source % inner)
            slot = high ^ (source // inner)
            place = (j * per_col + b) * width
            for k in range(inner):

                @pl.when((block == k) & (slot < first))
                def _():
                    at = pl.multiple_of(slot * width, width)
                    picked[:, place : place + width] = s_refs[2 * k][:, pl.ds(at, width)]

                @pl.when((block == k) & (slot >= first))
                def _():
                    at = pl.multiple_of((slot - first) * width, width)
                    picked[:, place : place + width] = s_refs[2 * k + 1][:, pl.ds(at, width)]

    own = jnp.concatenate([s_refs[0][...], s_refs[1][...]], axis=1)
    value = cross_rows(own, picked[...])
    for j in range(cols):
        out_refs[j][...] = value[:, j * per_col * width : (j + 1) * per_col * width]


def split_kernel(*refs, outer):
    total = refs[0][...]
    for ref in refs[1:-outer]:
        total = total + ref[...]
    rows = total.shape[0] // outer
    for m in range(outer):
        refs[m - outer][...] = total[m * rows : (m + 1) * rows]


def round_kernel(*refs):
    total = refs[0][...]
    for ref in refs[1:-1]:
        total = total + ref[...]
    refs[-1][...] = total.astype(refs[-1].dtype)


def left_kernel(
    ids_ref, tiles_ref, ranks_ref, bands_ref, trail_ref, panel_ref, right_ref, out_ref, kept_ref, *, width
):
    own_tile = tiles_ref[ids_ref[3]]
    own_rank = ranks_ref[own_tile, own_tile]
    for b in range(bands_ref.shape[0]):
        stack = jnp.concatenate([trail_ref[0, b], panel_ref[0]], axis=1)
        mask = keep_mask(width, ranks_ref[own_tile, bands_ref[b]], own_rank)
        out_ref[0, b] = jnp.where(mask, cross_rows(stack, stack), 0.0)
        kept_ref[b] = jnp.where(
            mask[:width, :width], cross_rows(right_ref[0, b], right_ref[0, b]), 0.0
        )


def pick_kernel(ids_ref, sources_ref, *refs, inner, share):
    bands_refs, t_refs, out_refs = refs[:share], refs[share : share + inner], refs[share + inner :]
    for j in range(share):
        for b in range(bands_refs[j].shape[0]):
            block = ids_ref[1] ^ (sources_ref[j * bands_refs[0].shape[0] + b] % inner)
            for k in range(inner):

                @pl.when(block == k)
                def _():
                    out_refs[j][b] = t_refs[k][...]


def join_kernel(*refs):
    size = refs[0].shape[1]
    for j, ref in enumerate(refs[:-1]):
        refs[-1][:, j * size : (j + 1) * size] = ref[...]


def sort_kernel(ids_ref, own_ref, other_ref, kept_ref, sent_ref):
    same = (ids_ref[2] ^ ids_ref[4]) == 0

    @pl.when(same)
    def _():
        kept_ref[...] = own_ref[...]
        sent_ref[...] = other_ref[...]

    @pl.when(jnp.logical_not(same))
    def _():
        kept_ref[...] = other_ref[...]
        sent_ref[...] = own_ref[...]


def merge_kernel(ids_ref, sources_ref, bands_ref, kept_ref, got_ref, out_ref, *, inner, bit):
    for b in range(bands_ref.shape[0]):
        other = ((sources_ref[b] // inner) ^ ids_ref[0]) & bit

        @pl.when(other == 0)
        def _():
            out_ref[b] = kept_ref[b]

        @pl.when(other != 0)
        def _():
            out_ref[b] = got_ref[b]


def right_kernel(
    ids_ref, tiles_ref, ranks_ref, bands_ref, *refs, pieces, outer, width, share
):
    part_refs = refs[:outer]
    q_refs = refs[outer : outer + sum(pieces)]
    kept_ref, trail_ref, out_ref, stack = refs[outer + sum(pieces) :]
    low, flip = ids_ref[1], ids_ref[4] if share > 1 else 0
    own_tile = tiles_ref[ids_ref[3]]
    own_rank = ranks_ref[own_tile, own_tile]
    quarter = stack.shape[0] // len(pieces)
    per_col = bands_ref.shape[0]
    rows = lax.broadcasted_iota(jnp.int32, (width, width), 0)
    cols = lax.broadcasted_iota(jnp.int32, (width, width), 1)
    nothing = jnp.zeros((width, width), jnp.bfloat16)
    lines = []
    for b in range(per_col):
        band_tile = bands_ref[b]
        lanes = slice(b * width, (b + 1) * width)
        total = part_refs[0][:, lanes]
        for m in range(1, outer):
            total = total + part_refs[m][:, lanes]
        live = (rows < own_rank) & (cols < ranks_ref[band_tile, band_tile])
        live = live & (band_tile < own_tile)
        core_mat = jnp.where(live, total, 0.0).astype(jnp.bfloat16)
        lines.append(
            jnp.concatenate([core_mat if i == b else nothing for i in range(per_col)], axis=1)
        )
    core_all = jnp.concatenate(lines, axis=0)
    at = 0
    for k, count in enumerate(pieces):
        blocks = max(share, count)
        size = quarter // blocks
        for h in range(blocks):
            part, j = h * count // blocks, h * share // blocks
            own = pl.ds((h - part * blocks // count) * size, size)
            update = lax.dot_general(
                jnp.concatenate([q_refs[at + part][b, own, :] for b in range(per_col)], axis=1),
                core_all,
                (((1,), (1,)), ((), ())),
                preferred_element_type=jnp.float32,
            )
            inside = (flip ^ j) * (quarter // share) + (h - j * blocks // share) * size
            place = pl.multiple_of((low ^ k) * quarter + inside, 16)
            stack[pl.ds(place, size), :] = -update.astype(jnp.bfloat16)
        at += count
    for b in range(per_col):
        change = stack[:, b * width : (b + 1) * width]
        both = cross_rows(change, jnp.concatenate([trail_ref[0, b], change], axis=1))
        mixed = jnp.where(cols < ranks_ref[own_tile, bands_ref[b]], both[:, :width], 0.0)
        out_ref[0, b, :width, :width] = kept_ref[b]
        out_ref[0, b, :width, width:] = mixed.T
        out_ref[0, b, width:, :width] = mixed
        out_ref[0, b, width:, width:] = both[:, width:]


def call(kernel, outs, scalars, arrays, scratch=()):
    result = pl.pallas_call(
        kernel,
        out_shape=outs,
        in_specs=[SMEM] * len(scalars) + [VMEM] * len(arrays),
        out_specs=jax.tree.map(lambda _: VMEM, outs),
        scratch_shapes=scratch,
        compiler_params=pltpu.CompilerParams(vmem_limit_bytes=SCRATCH_BYTES),
    )(*scalars, *[pltpu.with_memory_space_constraint(x, pltpu.VMEM) for x in arrays])
    return list(result) if isinstance(outs, list) else result


def shards(panel_u, panel_v, linv, trail_u, trail_v, rank_map, tile_of_slot, band_cols, *, rows, cols):
    inner = 1
    while inner * inner < rows:
        inner *= 2
    outer = rows // inner
    points, width = panel_u.shape[1], panel_u.shape[2]
    per_col = band_cols.shape[0]
    block_rows = linv.shape[0]
    kept_rows = inner // cols * block_rows
    f32, bf16 = jnp.float32, jnp.bfloat16
    row = lax.axis_index("row").astype(jnp.int32)
    core = lax.axis_index("col").astype(jnp.int32)
    high, low = row // inner, row % inner
    halved = inner == 4 and outer == 4 and cols == 2
    ids = jnp.stack([high, low, core, row, high % 2 if halved else core])

    def swap(x, axis, distance, count):
        return lax.ppermute(x, axis, [(i, i ^ distance) for i in range(count)])

    def low_swap(x, k):
        return swap(x, "row", k, rows)

    def high_swap(x, m):
        return swap(x, "row", m * inner, rows)

    def core_swap(x, j):
        return swap(x, "col", j, cols)

    v_blocks = [panel_v[0]] + [None] * (outer - 1)
    for m in sorted(range(1, outer), key=lambda m: (m & (m - 1), -m)):
        low_bit = m & -m
        v_blocks[m] = lax.ppermute(
            v_blocks[m ^ low_bit], "row", [(r, r ^ (low_bit * inner)) for r in range(rows)]
        )
    if inner == 4:
        half = block_rows // 2
        x_block, y_block = low_swap(linv, 1), low_swap(linv, 2)
        far_first = lax.ppermute(y_block[:half], "row", [(r, r ^ 1) for r in range(rows)])
        far_second = lax.ppermute(x_block[half:], "row", [(r, r ^ 2) for r in range(rows)])
        l_blocks = [linv, x_block, y_block, far_first, far_second]
        pieces = (1, 1, 1, 2)
    else:
        l_blocks = [linv] + [low_swap(linv, k) for k in range(1, inner)]
        pieces = (1,) * inner
    bands = [band_cols] + [core_swap(band_cols, j) for j in range(1, cols)]
    sources = pl.pallas_call(
        table_kernel,
        out_shape=jax.ShapeDtypeStruct((cols * per_col,), jnp.int32),
        in_specs=[SMEM] * (1 + cols),
        out_specs=SMEM,
        name="table",
    )(tile_of_slot, *bands)

    gram_left, gram_kept = call(
        functools.partial(left_kernel, width=width),
        [
            jax.ShapeDtypeStruct((1, per_col, 2 * width, 2 * width), f32),
            pltpu.VMEM((per_col, width, width), f32),
        ],
        (ids, tile_of_slot, rank_map, band_cols),
        (trail_u, panel_u, trail_v),
    )

    quarter = points // inner
    share = cols if quarter % (cols * 16) == 0 else 1
    size = quarter // share
    split_rows = halved and share == 2
    mine = core * size if share > 1 else 0
    t_blocks = [
        lax.dynamic_slice_in_dim(panel_u[0], (low ^ k) * quarter + mine, size)
        for k in range(inner)
    ]
    t_blocks = t_blocks[:1] + [low_swap(t_blocks[k], k) for k in range(1, inner)]
    picked = call(
        functools.partial(pick_kernel, inner=inner, share=share),
        [pltpu.VMEM((per_col, size, width), bf16)] * share,
        (ids, sources, *bands[:share]),
        t_blocks,
    )

    def merged(kept, got, bit):
        return call(
            functools.partial(merge_kernel, inner=inner, bit=bit),
            pltpu.VMEM(kept.shape, bf16),
            (ids, sources, band_cols),
            (kept, got),
        )

    base = picked[0]
    exchanged = picked[:1] + [core_swap(picked[j], j) for j in range(1, share)]
    if split_rows:
        kept, sent = call(
            sort_kernel, [pltpu.VMEM((per_col, size, width), bf16)] * 2, (ids,), exchanged
        )
        kept = merged(kept, high_swap(sent, 1), 1)
        kept = merged(kept, high_swap(kept, 2), 2)
        rest = high_swap(kept, 1)
        kept_y, rest_x = low_swap(kept, 2), low_swap(rest, 1)
        kept_x, rest_y = low_swap(kept, 1), low_swap(rest, 2)
        far = [swap(kept_y, "row", 1, rows), swap(rest_x, "row", 2, rows)]
        base_blocks = [kept, rest, kept_x, rest_x, kept_y, rest_y, *far]
        base_pieces = (2,) * inner
    else:
        if share > 1:
            base = call(join_kernel, pltpu.VMEM((per_col, quarter, width), bf16), (), exchanged)
        bit = outer // 2
        while bit:
            base = merged(base, high_swap(base, bit), bit)
            bit //= 2
        base_blocks = [base] + [low_swap(base, k) for k in range(1, inner)]
        base_pieces = (1,) * inner

    early = outer - 1
    solved_blocks = []
    for slots in (v_blocks[:early], v_blocks[early:]):
        lanes = len(slots) * width
        parts = call(
            functools.partial(solve_kernel, pieces=pieces, cols=cols),
            [pltpu.VMEM((kept_rows, lanes), f32)] * cols,
            (ids,),
            (*l_blocks, *slots),
        )
        solved = call(
            round_kernel,
            pltpu.VMEM((kept_rows, lanes), bf16),
            (),
            parts[:1] + [core_swap(parts[j], j) for j in range(1, cols)],
        )
        solved_blocks.append([solved] + [low_swap(solved, k) for k in range(1, inner)])
    cores = call(
        functools.partial(core_kernel, inner=inner, cols=cols, width=width, first=early),
        [pltpu.VMEM((outer * width, per_col * width), f32)] * cols,
        (ids, sources, *bands),
        [block for pair in zip(*solved_blocks) for block in pair],
        [pltpu.VMEM((kept_rows, cols * per_col * width), bf16)],
    )
    core_parts = call(
        functools.partial(split_kernel, outer=outer),
        [pltpu.VMEM((width, per_col * width), f32)] * outer,
        (),
        cores[:1] + [core_swap(cores[j], j) for j in range(1, cols)],
    )
    core_parts = core_parts[:1] + [high_swap(core_parts[m], m) for m in range(1, outer)]

    gram_right = call(
        functools.partial(right_kernel, pieces=base_pieces, outer=outer, width=width, share=share),
        jax.ShapeDtypeStruct((1, per_col, 2 * width, 2 * width), f32),
        (ids, tile_of_slot, rank_map, band_cols),
        (*core_parts, *base_blocks, gram_kept, trail_v),
        [pltpu.VMEM((points, per_col * width), bf16)],
    )
    return gram_left, gram_right


def solution(mesh):
    rows, cols = mesh.shape["row"], mesh.shape["col"]

    def body(*args):
        return shards(*args, rows=rows, cols=cols)

    return jax.shard_map(
        body,
        mesh=mesh,
        in_specs=(
            P("row", None, None),
            P("row", "col", None),
            P("row", "col"),
            P("row", "col", None, None),
            P("row", "col", None, None),
            P(),
            P(),
            P("col"),
        ),
        out_specs=(P("row", "col", None, None), P("row", "col", None, None)),
        check_vma=False,
    )
```
